256 devices in a mesh: feat: 16 (over z, y_hi), ex: 16 (over y_lo, x, core).
Axes of the slice: x: 4, y: 4 (y_hi: 2, y_lo: 2; y = y_hi * 2 + y_lo), z: 8, core: 2. Of those that a mesh axis runs over, the one named last changes fastest.
Arguments:
- activations: bfloat16 [1024, 28672], P('ex', 'feat'), may hold values from -6 to 6
- out_grads: bfloat16 [1024, 8192], P('feat', 'ex'), may hold values from -6 to 6
- basis_in: bfloat16 [28672, 28672], P('feat', 'ex'), may hold values from -0.03125 to 0.03125
- basis_out: bfloat16 [8192, 8192], P('ex', 'feat'), may hold values from -0.0625 to 0.0625
Outputs:
- correction: float32 [8192, 28672], P('feat', 'ex')
The draws below stay inside these ranges and needn't reach their ends.
All inputs are finite; a program needn't handle non-finite values.
Results may differ from the reference program's by a relative error of at most 0.0034.
Values may be sent and summed in bfloat16 or wider, within the bound.
A program may use at most 64 MiB of HBM per device.

```python
import jax
import jax.numpy as jnp
from jax import lax

DIN = 28672
DOUT = 8192
SEQ_LEN = 256
SEQS = 4
TOKENS = 1024


def level_of(rng, extent, pieces, smallest, top_value):
    level = 1.0
    for position, parts in pieces:
        heights = jax.random.uniform(jax.random.fold_in(jax.random.fold_in(rng, 6), position), (parts,), jnp.float32, smallest / len(pieces), top_value / len(pieces))
        level = level * jnp.repeat(jnp.exp(heights), extent[position] // parts).reshape((-1,) + (1,) * (len(extent) - 1 - position))
    return level


def bell_draw(rng, dims, width, most, split=(), held_as=jnp.bfloat16):
    gain = level_of(rng, dims, split, -0.22, 0.18) if split else 1.0
    entries = jax.random.normal(rng, dims, jnp.float32) * width * gain
    return jnp.minimum(jnp.maximum(entries, -most), most).astype(held_as)


def setup_inputs(seed: int = 0) -> dict:
    splits = jax.random.split(jax.random.key(seed), 5)
    activations = bell_draw(splits[0], (TOKENS, DIN), 1.0, 6.0, ((0, 16), (1, 16)))
    out_grads = bell_draw(splits[1], (TOKENS, DOUT), 1.0, 6.0, ((0, 16), (1, 16)))
    basis_in = bell_draw(splits[2], (DIN, DIN), DIN ** -0.5, 0.03125, ((0, 16), (1, 16)))
    basis_out = bell_draw(splits[3], (DOUT, DOUT), DOUT ** -0.5, 0.0625, ((0, 16), (1, 16)))
    return {"activations": activations, "out_grads": out_grads, "basis_in": basis_in, "basis_out": basis_out}


def reference(activations, out_grads, basis_in, basis_out):
    rotated_in = jnp.dot(activations, basis_in, preferred_element_type=jnp.float32).astype(jnp.bfloat16)
    rotated_out = jnp.dot(out_grads, basis_out, preferred_element_type=jnp.float32).astype(jnp.bfloat16)
    in_blocks = rotated_in.reshape(SEQS, SEQ_LEN, DIN)
    out_blocks = rotated_out.reshape(SEQS, SEQ_LEN, DOUT)

    def accumulate(total, pair):
        per_seq = jnp.dot(pair[0].T, pair[1], preferred_element_type=jnp.float32)
        return total + per_seq * per_seq, None

    total, unused = lax.scan(accumulate, jnp.zeros((DOUT, DIN), jnp.float32), (out_blocks, in_blocks))
    return total / jnp.float32(TOKENS)
```

```python
import functools

import jax
import jax.numpy as jnp
from jax import lax
from jax.experimental import pallas as pl
from jax.experimental.pallas import tpu as pltpu
from jax.sharding import PartitionSpec as P

SEQ_LEN = 256
BC = 256
MESH = pl.DeviceIdType.MESH
F32, BF16 = jnp.float32, jnp.bfloat16
NZ, NX = 8, 4
STOP = None


def kernel(sz, a_hbm, g_hbm, bi_hbm, bo_hbm, out_hbm, a_full, bi, part, sbuf, rbuf, tot, yrecv, rin, outv, g_full, bo,
           pout, sib, ro, rout, rout_t, a_ss, a_rs, gy_s, g_ss, g_rs, rs_ss, rs_rs, y_ss, y_rs, ag_ss, ag_rs,
           ob_s, oq_ss, oq_rs, ot_ss, ot_rs, of_ss, of_rs, lsem, out_sem):
    tk, nb = sz
    f, e = lax.axis_index("feat"), lax.axis_index("ex")
    z, yh = f // 2, f % 2
    ci, c = e // 2, e % 2
    yl, x = ci // NX, ci % NX
    yo, xm, xp, x2 = 1 - yl, (x + NX - 1) % NX, (x + 1) % NX, (x + 2) % NX
    t2 = 2 * tk

    def dev(z_=z, yh_=yh, yl_=yl, x_=x, c_=c):
        return {"feat": z_ * 2 + yh_, "ex": (yl_ * NX + x_) * 2 + c_}

    def send(src, dst, ss, rs, to):
        return pltpu.make_async_remote_copy(
            src_ref=src, dst_ref=dst, send_sem=ss, recv_sem=rs, device_id=to, device_id_type=MESH
        )

    zp, zm = dev(z_=(z + 1) % NZ), dev(z_=(z + NZ - 1) % NZ)
    sibling, ypair, yhpair = dev(c_=1 - c), dev(yl_=yo), dev(yh_=1 - yh)
    xpd, xmd = dev(x_=xp), dev(x_=xm)

    def chip(d):
        k = (ci + d) % (2 * NX)
        return k, {"feat": f, "ex": k * 2 + c}

    barrier = pltpu.get_barrier_semaphore()
    others = [zp, zm, sibling, yhpair] + [chip(d)[1] for d in range(1, 2 * NX)]
    for to in others:
        pl.semaphore_signal(barrier, inc=1, device_id=to, device_id_type=MESH)

    ld_bi = pltpu.make_async_copy(bi_hbm, bi, lsem.at[0])
    ld_bo = pltpu.make_async_copy(bo_hbm, bo, lsem.at[1])

    def rows(yl_, x_, c_=c, off=0, size=tk):
        return pl.ds(pl.multiple_of(((yl_ * NX + x_) * 2 + c_) * tk + off, tk // 2), size)

    ld_a = pltpu.make_async_copy(a_hbm, a_full.at[rows(yl, x)], lsem.at[2])
    frow = pl.ds(pl.multiple_of(f * tk, tk), tk)
    ld_g = pltpu.make_async_copy(g_hbm, g_full.at[frow], lsem.at[3])
    for ld in (ld_a, ld_g, ld_bo, ld_bi):
        ld.start()
    pl.semaphore_wait(barrier, len(others))

    hk = tk // 2
    a_out = [
        (rows(yl, x), ypair), (rows(yl, x), xpd), (rows(yl, x), xmd),
        (rows(yl, xm, size=hk), xpd), (rows(yl, xp, off=hk, size=hk), xmd),
        (rows(yo, x), xpd), (rows(yo, x), xmd), (rows(yl, x2), ypair),
    ]
    a_in = [rows(yo, x), rows(yl, xm), rows(yl, xp), rows(yl, x2, size=hk), rows(yl, x2, off=hk, size=hk),
            rows(yo, xm), rows(yo, xp), rows(yo, x2)]
    shards = [(yl, x), (yl, xm), (yl, xp), (yo, x), (yo, xm), (yo, xp), (yl, x2), (yo, x2)]
    for s in shards:
        a_out.append((rows(*s), sibling))
        a_in.append(rows(*s, c_=1 - c))

    def a_msg(i):
        r, to = a_out[i]
        src = a_hbm if i in (0, 1, 2, 8) else a_full.at[r]
        return send(src, a_full.at[r], a_ss.at[i], a_rs.at[i], to)

    def a_wait(i):
        r = a_full.at[a_in[i]]
        send(r, r, a_ss.at[i], a_rs.at[i], a_out[i][1]).wait_recv()

    def ag_region(ref, s, way, incoming):
        o = (z + NZ - s + (0 if incoming else 1)) if way == 0 else (z + s - (0 if incoming else 1))
        start = (o % NZ) * t2
        if s == 4:
            return ref.at[pl.ds(pl.multiple_of(start + way * tk, tk), tk)]
        return ref.at[pl.ds(pl.multiple_of(start, t2), t2)]

    def ag_send(ref, s, way, ss, rs):
        r = ag_region(ref, s, way, False)
        return send(r, r, ss.at[way, s - 1], rs.at[way, s - 1], zm if way else zp)

    def ag_wait(ref, s, way, ss, rs):
        r = ag_region(ref, s, way, True)
        send(r, r, ss.at[way, s - 1], rs.at[way, s - 1], zm if way else zp).wait_recv()

    gy = send(g_hbm, g_full.at[frow], gy_s.at[0], gy_s.at[1], yhpair)
    gy.start()
    for i in (0, 1, 2, 8):
        a_msg(i).start()
    orow = pl.ds(pl.multiple_of((z * 2 + 1 - yh) * tk, tk), tk)
    send(g_full.at[orow], g_full.at[orow], gy_s.at[0], gy_s.at[1], yhpair).wait_recv()
    ld_g.wait()

    def g_step(s):
        for way in (0, 1):
            if s > 1:
                ag_wait(g_full, s - 1, way, g_ss, g_rs)
            if s <= 4:
                ag_send(g_full, s, way, g_ss, g_rs).start()

    g_step(1)
    a_wait(1), a_msg(3).start(), a_msg(9).start()
    a_wait(2), a_msg(4).start(), a_msg(10).start()
    a_wait(0), a_msg(5).start(), a_msg(6).start(), a_msg(11).start()
    g_step(2)
    a_wait(3), a_wait(4), a_msg(7).start(), a_msg(14).start()
    g_step(3)
    a_wait(5), a_msg(12).start()
    a_wait(6), a_msg(13).start()
    g_step(4)
    a_wait(7), a_msg(15).start()
    ld_a.wait()
    for i in range(8, 16):
        a_wait(i)
    ld_bi.wait()

    def own(b, o):
        return part[b, pl.ds(pl.multiple_of((o % NZ) * t2, t2), t2), :]

    def rs_size(s):
        return pl.ds(0, tk if s == 1 else t2)

    def rs_copy(b, s, way):
        r = rs_size(s)
        return send(
            sbuf.at[b, way, s - 1, r], rbuf.at[b, way, s - 1, r], rs_ss.at[b, way, s - 1], rs_rs.at[b, way, s - 1],
            zm if way else zp,
        )

    def rs_first(b):
        start = ((z + 4) % NZ) * t2
        for way in (0, 1):
            r = pl.ds(pl.multiple_of(start + way * tk, tk), tk)
            sbuf[b, way, 0, rs_size(1), :] = part[b, r, :].astype(BF16)
            rs_copy(b, 1, way).start()

    def rs_next(b, s):
        for way in (0, 1):
            rs_copy(b, s - 1, way).wait_recv()
            mine = own(b, z + NZ - (5 - s) if way else z + (5 - s))
            if s == 2:
                got = rbuf[b, way, 0, rs_size(1), :].astype(F32)
                there = slice(way * tk, way * tk + tk)
                rest = slice((1 - way) * tk, (1 - way) * tk + tk)
                sbuf[b, way, 1, there, :] = (mine[there] + got).astype(BF16)
                sbuf[b, way, 1, rest, :] = mine[rest].astype(BF16)
            else:
                sbuf[b, way, s - 1] = (mine + rbuf[b, way, s - 2].astype(F32)).astype(BF16)
            rs_copy(b, s, way).start()

    def y_copy(b):
        return send(tot.at[b], yrecv.at[b], y_ss.at[b], y_rs.at[b], yhpair)

    def rs_last(b):
        for way in (0, 1):
            rs_copy(b, 4, way).wait_recv()
        tot[b] = own(b, z) + rbuf[b, 0, 3].astype(F32) + rbuf[b, 1, 3].astype(F32)
        y_copy(b).start()

    def ag_step(b, s):
        for way in (0, 1):
            if s > 1:
                ag_wait(rin.at[b], s - 1, way, ag_ss.at[b], ag_rs.at[b])
            if s <= 4:
                ag_send(rin.at[b], s, way, ag_ss.at[b], ag_rs.at[b]).start()

    def y_last(b):
        y_copy(b).wait_recv()
        rin[b, pl.ds(pl.multiple_of(z * t2, t2), t2), :] = (tot[b] + yrecv[b]).astype(BF16)
        ag_step(b, 1)

    def out_copy(b):
        cols = pl.ds(pl.multiple_of(b * BC, BC), BC)
        return pltpu.make_async_copy(outv.at[b], out_hbm.at[:, cols], out_sem.at[b])

    def correction(b):
        ag_step(b, 5)
        total = None
        for n in range(rout_t.shape[1] // SEQ_LEN):
            per_seq = jnp.dot(
                rout_t[:, n * SEQ_LEN : (n + 1) * SEQ_LEN],
                rin[b, n * SEQ_LEN : (n + 1) * SEQ_LEN, :],
                preferred_element_type=F32,
            )
            total = per_seq * per_seq if total is None else total + per_seq * per_seq
        outv[b] = total
        out_copy(b).start()

    ob = send(pout.at[1 - c], sib, ob_s.at[0], ob_s.at[1], sibling)

    def out_partial():
        g_step(5)
        ld_bo.wait()
        per = 4 * tk
        for m in range(g_full.shape[0] // per):
            val = jnp.dot(g_full[m * per : (m + 1) * per, :], bo[...], preferred_element_type=F32)
            for k in range(4):
                pout[k % 2, 2 * m + k // 2] = val[k * tk : (k + 1) * tk]
        ob.start()

    def oq_copy(d):
        k, to = chip(d)
        return send(pout.at[c, k], ro.at[ci], oq_ss.at[d], oq_rs.at[d], to)

    def out_pair():
        ob.wait_recv()
        for k in range(2 * NX):
            pout[c, k] = pout[c, k] + sib[k]
        for d in range(1, 2 * NX):
            oq_copy(d).start()

    def erow(k, c_):
        return pl.ds(pl.multiple_of((k * 2 + c_) * tk, tk), tk)

    def ot_copy(d):
        r = rout.at[erow(ci, c)]
        return send(r, r, ot_ss.at[d], ot_rs.at[d], chip(d)[1])

    def of_copy(d):
        r = rout.at[erow((ci + 2 * NX - d) % (2 * NX), c)]
        return send(r, r, of_ss.at[d], of_rs.at[d], sibling)

    def out_sum():
        total = pout[c, ci]
        for d in range(1, 2 * NX):
            k = (ci + 2 * NX - d) % (2 * NX)
            send(ro.at[k], ro.at[k], oq_ss.at[d], oq_rs.at[d], chip(d)[1]).wait_recv()
            total = total + ro[k]
        rout[erow(ci, c), :] = total.astype(BF16)
        for d in range(1, 2 * NX):
            ot_copy(d).start()
        of_copy(0).start()

    def out_forward():
        for d in range(1, 2 * NX):
            r = rout.at[erow((ci + 2 * NX - d) % (2 * NX), c)]
            send(r, r, ot_ss.at[d], ot_rs.at[d], chip(d)[1]).wait_recv()
            of_copy(d).start()

    def out_done():
        for d in range(2 * NX):
            r = rout.at[erow((ci + 2 * NX - d) % (2 * NX), 1 - c)]
            send(r, r, of_ss.at[d], of_rs.at[d], sibling).wait_recv()
        for m in range(rout.shape[0] // SEQ_LEN):
            rout_t[:, m * SEQ_LEN : (m + 1) * SEQ_LEN] = rout[m * SEQ_LEN : (m + 1) * SEQ_LEN, :].T

    out_phase = {2: out_partial, 3: out_pair, 5: out_sum, 7: out_forward, 8: out_done}

    def slot(t, carry):
        def block(lag, run):
            b = t - lag

            @pl.when((b >= 0) & (b < nb))
            def _():
                run(jnp.clip(b, 0, nb - 1))

        def product(b):
            cols = pl.ds(pl.multiple_of(b * BC, BC), BC)
            part[b] = jnp.dot(a_full[...], bi[:, cols], preferred_element_type=F32)
            rs_first(b)

        block(0, product)
        for lag in (1, 2, 3):
            block(lag, functools.partial(rs_next, s=lag + 1))
        block(4, rs_last)
        for at, run in out_phase.items():
            pl.when(t == at)(run)
        block(5, y_last)
        for lag in (6, 7, 8):
            block(lag, functools.partial(ag_step, s=lag - 4))
        block(9, correction)
        return carry

    lax.fori_loop(0, nb + 9, slot, 0)

    for i in range(16):
        a_msg(i).wait_send()
    gy.wait_send()
    ob.wait_send()
    for s in range(1, 5):
        for way in (0, 1):
            ag_send(g_full, s, way, g_ss, g_rs).wait_send()
    for d in range(2 * NX):
        of_copy(d).wait_send()
        if d:
            oq_copy(d).wait_send()
            ot_copy(d).wait_send()

    def drain(b, carry):
        for s in range(1, 5):
            for way in (0, 1):
                rs_copy(b, s, way).wait_send()
                ag_send(rin.at[b], s, way, ag_ss.at[b], ag_rs.at[b]).wait_send()
        y_copy(b).wait_send()
        out_copy(b).wait()
        return carry

    lax.fori_loop(0, nb, drain, 0)


def per_device(activations, out_grads, basis_in, basis_out):
    tk, kin = activations.shape
    kout, nout = basis_out.shape
    nin = basis_in.shape[1]
    nb, tokens = nin // BC, tk * 16
    dma, vmem = pltpu.SemaphoreType.DMA, pltpu.VMEM
    squares = pl.pallas_call(
        functools.partial(kernel, (tk, nb)),
        out_shape=jax.ShapeDtypeStruct((nout, nin), F32),
        in_specs=[pl.BlockSpec(memory_space=pl.ANY)] * 4,
        out_specs=pl.BlockSpec(memory_space=pl.ANY),
        scratch_shapes=[
            vmem((tokens, kin), BF16),
            vmem((kin, nin), BF16),
            vmem((nb, tokens, BC), F32),
            vmem((nb, 2, 4, 2 * tk, BC), BF16),
            vmem((nb, 2, 4, 2 * tk, BC), BF16),
            vmem((nb, 2 * tk, BC), F32),
            vmem((nb, 2 * tk, BC), F32),
            vmem((nb, tokens, BC), BF16),
            vmem((nb, nout, BC), F32),
            vmem((tokens, kout), BF16),
            vmem((kout, nout), BF16),
            vmem((2, 8, tk, nout), F32),
            vmem((8, tk, nout), F32),
            vmem((8, tk, nout), F32),
            vmem((tokens, nout), BF16),
            vmem((nout, tokens), BF16),
            dma((16,)), dma((16,)), dma((2,)), dma((2, 4)), dma((2, 4)),
            dma((nb, 2, 4)), dma((nb, 2, 4)), dma((nb,)), dma((nb,)), dma((nb, 2, 4)), dma((nb, 2, 4)),
            dma((2,)), dma((8,)), dma((8,)), dma((8,)), dma((8,)), dma((8,)), dma((8,)), dma((4,)), dma((nb,)),
        ],
        compiler_params=pltpu.CompilerParams(
            collective_id=0, has_side_effects=True, vmem_limit_bytes=60 * 1024 * 1024
        ),
    )(activations, out_grads, basis_in, basis_out)
    return squares / jnp.float32(tokens)


def solution(mesh):
    return jax.shard_map(
        per_device,
        mesh=mesh,
        in_specs=(P("ex", "feat"), P("feat", "ex"), P("feat", "ex"), P("ex", "feat")),
        out_specs=P("feat", "ex"),
        check_vma=False,
    )
```

```python
import functools

import jax
import jax.numpy as jnp
from jax import lax
from jax.experimental import pallas as pl
from jax.experimental.pallas import tpu as pltpu
from jax.sharding import PartitionSpec as P

SEQ_LEN = 256
BC = 256
NG = 1
MESH = pl.DeviceIdType.MESH
F32, BF16 = jnp.float32, jnp.bfloat16
NZ, NX = 8, 4
Y_ITEMS = (0, 1, 2, 4, 5)
ORDER = (
    (0, 0, -1), (2, 0, 1), (1, 0, 0), (2, 0, 2), (0, 0, 1), (0, 0, 2), (2, 0, 3), (0, 0, 0), (2, 1, 1), (2, 0, 4),
    (0, 0, 4), (2, 1, 2), (2, 1, 3), (0, 0, 5), (0, 0, 6), (0, 0, 7), (2, 1, 4), (0, 0, 8), (4, 0, 0), (4, 1, 0), (4, 2, 0),
    (3, 1, 0), (4, 0, 1), (4, 3, 0), (4, 0, 2), (3, 2, 0), (4, 1, 1), (4, 3, 1), (4, 4, 0), (4, 1, 2), (4, 0, 3), (4, 3, 2),
    (4, 2, 1), (4, 5, 0), (4, 0, 4), (4, 2, 2), (4, 1, 3), (4, 6, 0), (4, 0, 5), (4, 4, 1), (4, 1, 4), (3, 3, 0), (4, 2, 3),
    (4, 0, 6), (4, 6, 1), (4, 4, 2), (4, 1, 5), (4, 5, 1), (4, 2, 4), (4, 0, 7), (4, 3, 3), (4, 6, 2), (3, 4, 0), (4, 4, 3),
    (4, 1, 6), (4, 5, 2), (4, 2, 5), (4, 0, 8), (4, 3, 4), (4, 6, 3), (4, 4, 4), (3, 5, 0), (4, 1, 7), (4, 5, 3), (4, 2, 6),
    (4, 0, 9), (4, 6, 4), (4, 4, 5), (4, 1, 8), (4, 3, 5), (4, 5, 4), (4, 2, 7), (3, 6, 0), (4, 4, 6), (4, 1, 9), (3, 7, 0),
    (4, 3, 6), (4, 2, 8), (4, 0, 10), (5, 0, 0), (4, 4, 7), (4, 5, 5), (4, 6, 5), (4, 3, 7), (4, 2, 9), (4, 4, 8),
    (4, 5, 6), (4, 6, 6), (4, 1, 10), (5, 1, 0), (4, 3, 8), (4, 4, 9), (4, 5, 7), (4, 6, 7), (4, 2, 10), (5, 2, 0),
    (4, 5, 8), (4, 3, 9), (5, 3, 0), (4, 6, 8), (4, 4, 10), (4, 5, 9), (5, 4, 0), (4, 6, 9), (5, 6, 0), (4, 5, 10),
    (5, 5, 0),
)


def kernel(dims, a_hbm, g_hbm, bi_hbm, bo_hbm, out, a_full, bi, part, sbuf, rbuf, ysend, yrecv, tot, ytot, rin, g_full, bo,
           pout, sib, ro, oy, rout, rout_t, a_ss, a_rs, gy_s, g_ss, g_rs, rs_ss, rs_rs, y_ss, y_rs, ag_ss, ag_rs, fy_ss, fy_rs,
           ob_s, oy_s, oq_ss, oq_rs, ot_ss, ot_rs, of_ss, of_rs, lsem):
    tg, nb = dims
    tk = tg // NG
    ni = nb * NG
    f, e = lax.axis_index("feat"), lax.axis_index("ex")
    z, yh = f // 2, f % 2
    ci, c = e // 2, e % 2
    yl, x = ci // NX, ci % NX
    yo, xm, xp, x2 = 1 - yl, (x + NX - 1) % NX, (x + 1) % NX, (x + 2) % NX
    t2 = 2 * tk

    def dev(z_=z, yh_=yh, yl_=yl, x_=x, c_=c):
        return {"feat": z_ * 2 + yh_, "ex": (yl_ * NX + x_) * 2 + c_}

    def send(src, dst, ss, rs, to):
        return pltpu.make_async_remote_copy(
            src_ref=src, dst_ref=dst, send_sem=ss, recv_sem=rs, device_id=to, device_id_type=MESH
        )

    zp, zm = dev(z_=(z + 1) % NZ), dev(z_=(z + NZ - 1) % NZ)
    zdev = (zp, zm)
    sibling, ypair, yhpair = dev(c_=1 - c), dev(yl_=yo), dev(yh_=1 - yh)
    xpd, xmd = dev(x_=xp), dev(x_=xm)

    barrier = pltpu.get_barrier_semaphore()
    others = [zp, zm, sibling, ypair, yhpair, xpd, xmd, dev(x_=x2)]
    for to in others:
        pl.semaphore_signal(barrier, inc=1, device_id=to, device_id_type=MESH)

    def rows(yl_, x_, c_=c, off=0, size=tk):
        return pl.ds(pl.multiple_of(((yl_ * NX + x_) * 2 + c_) * tk + off, tk // 2), size)

    def half(ref, n, way):
        return ref.at[pl.ds(way * (n // 2), n // 2)]

    ld_bi = pltpu.make_async_copy(bi_hbm, bi, lsem.at[0])
    ld_bo = pltpu.make_async_copy(bo_hbm, bo, lsem.at[1])
    ld_g = pltpu.make_async_copy(g_hbm, g_full.at[z, yh], lsem.at[2])
    ld_a = [
        pltpu.make_async_copy(a_hbm.at[pl.ds(h * tk, tk)], a_full.at[h, rows(yl, x)], lsem.at[3 + h]) for h in range(NG)
    ]
    for ld in (*ld_a, ld_g, ld_bo, ld_bi):
        ld.start()
    pl.semaphore_wait(barrier, len(others))

    hk = tk // 2
    a_out = [
        (rows(yl, x), ypair), (rows(yl, x), xpd), (rows(yl, x), xmd),
        (rows(yl, xm, size=hk), xpd), (rows(yl, xp, off=hk, size=hk), xmd),
        (rows(yo, x), xpd), (rows(yo, x), xmd), (rows(yl, x2), ypair),
    ]
    a_in = [rows(yo, x), rows(yl, xm), rows(yl, xp), rows(yl, x2, size=hk), rows(yl, x2, off=hk, size=hk),
            rows(yo, xm), rows(yo, xp), rows(yo, x2)]
    for s in [(yl, x), (yl, xm), (yl, xp), (yo, x), (yo, xm), (yo, xp), (yl, x2), (yo, x2)]:
        a_out.append((rows(*s), sibling))
        a_in.append(rows(*s, c_=1 - c))

    def a_msg(h, i):
        r, to = a_out[i]
        src = a_hbm.at[pl.ds(h * tk, tk)] if i in (0, 1, 2, 8) else a_full.at[h, r]
        return send(src, a_full.at[h, r], a_ss.at[h, i], a_rs.at[h, i], to)

    def a_wait(h, i, *then):
        r = a_full.at[h, a_in[i]]
        send(r, r, a_ss.at[h, i], a_rs.at[h, i], a_out[i][1]).wait_recv()
        for k in then:
            a_msg(h, k).start()

    def a_first(h):
        for i in (1, 2, 0, 8):
            a_msg(h, i).start()

    def a_done(h):
        ld_a[h].wait()
        for i in range(8, 16):
            a_wait(h, i)

    def ag_region(view, n, s, way, incoming):
        o = (z + NZ - s + (0 if incoming else 1)) if way == 0 else (z + s - (0 if incoming else 1))
        r = view(o % NZ)
        return half(r, n, way) if s == 4 else r

    def ag_copy(view, n, s, way, ss, rs, incoming=False):
        r = ag_region(view, n, s, way, incoming)
        return send(r, r, ss.at[way, s - 1], rs.at[way, s - 1], zdev[way])

    def ag_wait(view, n, s, way, ss, rs):
        ag_copy(view, n, s, way, ss, rs, True).wait_recv()

    def g_args(k):
        j = yh if k == 0 else 1 - yh
        return (lambda o: g_full.at[o, j]), tg, g_ss.at[k], g_rs.at[k]

    def g_copy(k, s, way):
        view, n, ss, rs = g_args(k)
        if k == 0 and s == 1:
            return send(g_hbm, view(z), ss.at[way, 0], rs.at[way, 0], zdev[way])
        return ag_copy(view, n, s, way, ss, rs)

    def g_step(k, s):
        view, n, ss, rs = g_args(k)
        for way in (0, 1):
            if s > 1:
                ag_wait(view, n, s - 1, way, ss, rs)
            if s <= 4:
                g_copy(k, s, way).start()

    gy = send(g_hbm, g_full.at[z, yh], gy_s.at[0], gy_s.at[1], yhpair)

    def is_y(i):
        return functools.reduce(jnp.logical_or, [i == k for k in Y_ITEMS])

    def zsize(kind):
        return t2 if kind == 0 else tk

    def mine(kind, i, o):
        if kind == 0:
            return part[i, o % NZ]
        return part[i, o % NZ, pl.ds(pl.multiple_of(yh * tk, tk), tk), :]

    def rs_copy(kind, i, s, way):
        n = zsize(kind)
        r = pl.ds(0, n // 2 if s == 1 else n)
        return send(
            sbuf.at[i, way, s - 1, r], rbuf.at[i, way, s - 1, r], rs_ss.at[i, way, s - 1], rs_rs.at[i, way, s - 1], zdev[way]
        )

    def rs_first(kind, i):
        n = zsize(kind)
        whole = mine(kind, i, z + 4)
        for way in (0, 1):
            sbuf[i, way, 0, pl.ds(0, n // 2), :] = whole[way * (n // 2) : (way + 1) * (n // 2)].astype(BF16)
            rs_copy(kind, i, 1, way).start()

    def rs_next(kind, i, s):
        n = zsize(kind)
        m = n // 2
        for way in (0, 1):
            rs_copy(kind, i, s - 1, way).wait_recv()
            own = mine(kind, i, z + NZ - (5 - s) if way else z + (5 - s))
            if s == 2:
                got = rbuf[i, way, 0, pl.ds(0, m), :].astype(F32)
                sbuf[i, way, 1, pl.ds(way * m, m), :] = (own[way * m : (way + 1) * m] + got).astype(BF16)
                sbuf[i, way, 1, pl.ds((1 - way) * m, m), :] = own[(1 - way) * m : (2 - way) * m].astype(BF16)
            else:
                got = rbuf[i, way, s - 2, pl.ds(0, n), :].astype(F32)
                sbuf[i, way, s - 1, pl.ds(0, n), :] = (own + got).astype(BF16)
            rs_copy(kind, i, s, way).start()

    def rs_last(kind, i):
        n = zsize(kind)
        for way in (0, 1):
            rs_copy(kind, i, 4, way).wait_recv()
        got = [rbuf[i, way, 3, pl.ds(0, n), :].astype(F32) for way in (0, 1)]
        return mine(kind, i, z) + got[0] + got[1]

    def view(kind, i):
        if kind == 0:
            return lambda o: rin.at[i, o]
        return lambda o: rin.at[i, o, pl.ds(pl.multiple_of(yh * tk, tk), tk)]

    def ag_step(kind, i, s):
        n = zsize(kind)
        for way in (0, 1):
            if s > 1:
                ag_wait(view(kind, i), n, s - 1, way, ag_ss.at[i], ag_rs.at[i])
            if s <= 4:
                ag_copy(view(kind, i), n, s, way, ag_ss.at[i], ag_rs.at[i]).start()
            if kind == 1 and s > 1:
                fy_copy(i, s - 1, way).start()
        if kind == 1 and s == 1:
            fy_copy(i, 0, 0).start()

    def y_copy(i):
        return send(tot.at[i], ytot.at[i], y_ss.at[i], y_rs.at[i], yhpair)

    def z_last(i):
        tot[i] = rs_last(0, i)
        y_copy(i).start()

    def z_sum(i):
        y_copy(i).wait_recv()
        rin[i, z] = (tot[i] + ytot[i]).astype(BF16)
        ag_step(0, i, 1)

    def yp_copy(i):
        return send(ysend.at[i], yrecv.at[i], y_ss.at[i], y_rs.at[i], yhpair)

    def y_start(i):
        other = pl.ds(pl.multiple_of((1 - yh) * tk, tk), tk)
        for o in range(NZ):
            ysend[i, o] = part[i, o, other, :].astype(BF16)
        yp_copy(i).start()

    def y_sum(i):
        yp_copy(i).wait_recv()
        own = pl.ds(pl.multiple_of(yh * tk, tk), tk)
        for o in range(NZ):
            part[i, o, own, :] = part[i, o, own, :] + yrecv[i, o].astype(F32)
        rs_first(1, i)

    def y_last(i):
        rin[i, z, pl.ds(pl.multiple_of(yh * tk, tk), tk), :] = rs_last(1, i).astype(BF16)
        ag_step(1, i, 1)

    def fy_region(i, s, way, j):
        r = rin.at[i, ((z + s) if way else (z + NZ - s)) % NZ, pl.ds(pl.multiple_of(j * tk, tk), tk)]
        return half(r, tk, way) if s == 4 else r

    def fy_copy(i, s, way, incoming=False):
        r = fy_region(i, s, way, 1 - yh if incoming else yh)
        return send(r, r, fy_ss.at[i, s, way], fy_rs.at[i, s, way], yhpair)

    fy_all = [(0, 0)] + [(s, way) for s in range(1, 5) for way in (0, 1)]

    def y_done(i):
        for s, way in fy_all:
            fy_copy(i, s, way, True).wait_recv()

    def correction(b):
        cols = pl.ds(pl.multiple_of(b * BC, BC), BC)
        total = None
        spans = 2 * SEQ_LEN // (tg * 2)
        for n in range(rout_t.shape[1] // SEQ_LEN):
            parts = [
                rin[h * nb + b, n * (spans // 2) + k] for h in range(NG) for k in range(spans // 2)
            ]
            per_seq = jnp.dot(
                rout_t[:, n * SEQ_LEN : (n + 1) * SEQ_LEN],
                jnp.concatenate(parts, axis=0),
                preferred_element_type=F32,
            )
            total = per_seq * per_seq if total is None else total + per_seq * per_seq
        out[:, cols] = total

    ob = send(pout.at[1 - c], sib, ob_s.at[0], ob_s.at[1], sibling)

    def out_partial():
        g_step(0, 5)
        g_step(1, 5)
        ld_g.wait()
        ld_bo.wait()
        for m in range(NZ // 2):
            grads = g_full[2 * m : 2 * m + 2].reshape(4 * tg, g_full.shape[3])
            val = jnp.dot(grads, bo[...], preferred_element_type=F32)
            for k in range(4):
                at = 2 * m + k // 2
                pout[k % 2, at // NX, at % NX] = val[k * tg : (k + 1) * tg]
        ob.start()

    def xplace(d):
        return (x + NX + d) % NX

    def oq_copy(d):
        return send(pout.at[c, :, xplace(d)], ro.at[x], oq_ss.at[d], oq_rs.at[d], dev(x_=xplace(d)))

    def out_pair():
        ob.wait_recv()
        for row in (0, 1):
            for k in range(NX):
                pout[c, row, k] = pout[c, row, k] + sib[row, k]
        for d in range(1, NX):
            oq_copy(d).start()

    def oy_copy():
        return send(pout.at[c, yo, x], oy, oy_s.at[0], oy_s.at[1], ypair)

    def out_row():
        for d in range(1, NX):
            r = ro.at[xplace(-d)]
            send(r, r, oq_ss.at[d], oq_rs.at[d], xpd).wait_recv()
        for row in (0, 1):
            total = pout[c, row, x]
            for d in range(1, NX):
                total = total + ro[xplace(-d), row]
            pout[c, row, x] = total
        oy_copy().start()

    def piece(r, d, c_=c):
        row = yo if r else yl
        return rout.at[pl.ds(pl.multiple_of(((row * NX + xplace(-d)) * 2 + c_) * tg, tg), tg)]

    def ot_copy(r, d):
        src = piece(r, 0)
        return send(src, src, ot_ss.at[r, d], ot_rs.at[r, d], dev(x_=xplace(d)) if d else ypair)

    def ot_wait(r, d):
        dst = piece(r, d) if d else piece(1, 0)
        send(dst, dst, ot_ss.at[r, d], ot_rs.at[r, d], xpd).wait_recv()

    def of_copy(r, d, c_=c):
        src = piece(r, d, c_)
        return send(src, src, of_ss.at[r, d], of_rs.at[r, d], sibling)

    def out_sum():
        oy_copy().wait_recv()
        rout[pl.ds(pl.multiple_of(e * tg, tg), tg), :] = (pout[c, yl, x] + oy[...]).astype(BF16)
        for d in range(NX):
            ot_copy(0, d).start()
        of_copy(0, 0).start()

    def out_forward():
        ot_wait(0, 0)
        of_copy(1, 0).start()
        for d in range(1, NX):
            ot_copy(1, d).start()
        for d in range(1, NX):
            ot_wait(0, d)
            of_copy(0, d).start()

    def out_forward2():
        for d in range(1, NX):
            ot_wait(1, d)
            of_copy(1, d).start()

    def out_done():
        for r in (0, 1):
            for d in range(NX):
                of_copy(r, d, 1 - c).wait_recv()
        for n in range(rout.shape[0] // SEQ_LEN):
            seq = rout[n * SEQ_LEN : (n + 1) * SEQ_LEN, :]
            parts = [
                seq[k * tg + h * tk : k * tg + (h + 1) * tk] for h in range(NG) for k in range(SEQ_LEN // tg)
            ]
            rout_t[:, n * SEQ_LEN : (n + 1) * SEQ_LEN] = jnp.concatenate(parts, axis=0).T

    def product(i):
        b = i % nb
        if (4, i, 0) == first_item:
            ld_bi.wait()
        val = jnp.dot(a_full[i // nb], bi[:, b * BC : (b + 1) * BC], preferred_element_type=F32)
        part[i] = val.reshape(NZ, t2, BC)

    def activations(h, k):
        if k == -1:
            a_first(h)
        elif k == 4:
            a_wait(h, 3)
            a_wait(h, 4, 7, 14)
        elif k == 8:
            a_done(h)
        else:
            a_wait(h, k, *{1: (3, 9), 2: (4, 10), 0: (5, 6, 11), 5: (12,), 6: (13,), 7: (15,)}[k])

    def gradients(k, s):
        if (k, s) == (1, 1):
            r = g_full.at[z, 1 - yh]
            send(r, r, gy_s.at[0], gy_s.at[1], yhpair).wait_recv()
        g_step(k, s)

    def stage(i, k):
        if i in Y_ITEMS:
            if k == 0:
                product(i)
                y_start(i)
            elif k == 1:
                y_sum(i)
            elif k < 5:
                rs_next(1, i, k)
            elif k == 5:
                y_last(i)
            elif k < 10:
                ag_step(1, i, k - 4)
            else:
                y_done(i)
        elif k == 0:
            product(i)
            rs_first(0, i)
        elif k < 4:
            rs_next(0, i, k + 1)
        elif k == 4:
            z_last(i)
        elif k == 5:
            z_sum(i)
        else:
            ag_step(0, i, k - 4)

    out_phases = (out_partial, out_pair, out_row, out_sum, out_forward, out_forward2, out_done)
    first_item = next(op for op in ORDER if op[0] == 4)
    for op, p, q in ORDER:
        if op == 0:
            activations(p, q)
        elif op == 1:
            gy.start()
        elif op == 2:
            gradients(p, q)
        elif op == 3:
            out_phases[p - 1]()
        elif op == 4:
            stage(p, q)
        else:
            correction(p)

    gy.wait_send()
    ob.wait_send()
    for h in range(NG):
        for i in range(16):
            a_msg(h, i).wait_send()
    for k in (0, 1):
        for s in range(1, 5):
            for way in (0, 1):
                g_copy(k, s, way).wait_send()
    oy_copy().wait_send()
    for d in range(NX):
        for r in (0, 1):
            of_copy(r, d).wait_send()
            if d or r == 0:
                ot_copy(r, d).wait_send()
        if d:
            oq_copy(d).wait_send()

    def drain(i, carry):
        for kind in (0, 1):

            @pl.when(is_y(i) == (kind == 1))
            def _():
                for s in range(1, 5):
                    for way in (0, 1):
                        rs_copy(kind, i, s, way).wait_send()
                        ag_copy(view(kind, i), zsize(kind), s, way, ag_ss.at[i], ag_rs.at[i]).wait_send()
                if kind == 0:
                    y_copy(i).wait_send()
                else:
                    yp_copy(i).wait_send()
                    for s, way in fy_all:
                        fy_copy(i, s, way).wait_send()

        return carry

    lax.fori_loop(0, ni, drain, 0)


def per_device(activations, out_grads, basis_in, basis_out):
    tg, kin = activations.shape
    kout, nout = basis_out.shape
    nin = basis_in.shape[1]
    nb, tokens = nin // BC, tg * 16
    tk, ni = tg // NG, nb * NG
    dma, vmem = pltpu.SemaphoreType.DMA, pltpu.VMEM
    squares = pl.pallas_call(
        functools.partial(kernel, (tg, nb)),
        out_shape=jax.ShapeDtypeStruct((nout, nin), F32),
        in_specs=[pl.BlockSpec(memory_space=pl.ANY)] * 4,
        out_specs=pl.BlockSpec(memory_space=pltpu.VMEM),
        scratch_shapes=[
            vmem((NG, tokens // NG, kin), BF16),
            vmem((kin, nin), BF16),
            vmem((ni, NZ, 2 * tk, BC), F32),
            vmem((ni, 2, 4, 2 * tk, BC), BF16),
            vmem((ni, 2, 4, 2 * tk, BC), BF16),
            vmem((ni, NZ, tk, BC), BF16),
            vmem((ni, NZ, tk, BC), BF16),
            vmem((ni, 2 * tk, BC), F32),
            vmem((ni, 2 * tk, BC), F32),
            vmem((ni, NZ, 2 * tk, BC), BF16),
            vmem((NZ, 2, tg, kout), BF16),
            vmem((kout, nout), BF16),
            vmem((2, 2, NX, tg, nout), F32),
            vmem((2, NX, tg, nout), F32),
            vmem((NX, 2, tg, nout), F32),
            vmem((tg, nout), F32),
            vmem((tokens, nout), BF16),
            vmem((nout, tokens), BF16),
            dma((NG, 16)), dma((NG, 16)), dma((2,)), dma((2, 2, 4)), dma((2, 2, 4)),
            dma((ni, 2, 4)), dma((ni, 2, 4)), dma((ni,)), dma((ni,)), dma((ni, 2, 4)), dma((ni, 2, 4)),
            dma((ni, 5, 2)), dma((ni, 5, 2)),
            dma((2,)), dma((2,)), dma((NX,)), dma((NX,)), dma((2, NX)), dma((2, NX)), dma((2, NX)), dma((2, NX)), dma((3 + NG,)),
        ],
        compiler_params=pltpu.CompilerParams(
            collective_id=0, has_side_effects=True, vmem_limit_bytes=60 * 1024 * 1024
        ),
    )(activations, out_grads, basis_in, basis_out)
    return squares / jnp.float32(tokens)


def solution(mesh):
    return jax.shard_map(
        per_device,
        mesh=mesh,
        in_specs=(P("ex", "feat"), P("feat", "ex"), P("feat", "ex"), P("ex", "feat")),
        out_specs=P("feat", "ex"),
        check_vma=False,
    )
```

```python
import functools

import jax
import jax.numpy as jnp
from jax import lax
from jax.experimental import pallas as pl
from jax.experimental.pallas import tpu as pltpu
from jax.sharding import PartitionSpec as P

SEQ_LEN = 256
BC = 256
NG = 1
MESH = pl.DeviceIdType.MESH
F32, BF16 = jnp.float32, jnp.bfloat16
NZ, NX = 8, 4
Y_ITEMS = (1, 2, 3, 5, 6)
ORDER = (
    (0, 0, -1), (2, 0, 1), (1, 0, 0), (2, 0, 2), (0, 0, 1), (0, 0, 2), (2, 0, 3), (0, 0, 0), (2, 1, 1), (2, 0, 4),
    (0, 0, 4), (2, 1, 2), (2, 1, 3), (0, 0, 5), (0, 0, 6), (0, 0, 7), (2, 1, 4), (0, 0, 8), (4, 6, 0), (3, 1, 0), (4, 5, 0),
    (4, 4, 0), (4, 6, 1), (3, 2, 0), (4, 3, 0), (4, 6, 2), (4, 4, 1), (4, 2, 0), (4, 6, 3), (4, 5, 1), (4, 4, 2), (4, 1, 0),
    (4, 5, 2), (4, 3, 1), (4, 4, 3), (4, 6, 4), (4, 0, 0), (4, 3, 2), (4, 5, 3), (3, 3, 0), (4, 6, 5), (4, 2, 1), (4, 0, 1),
    (4, 3, 3), (4, 5, 4), (4, 4, 4), (4, 6, 6), (4, 2, 2), (4, 0, 2), (4, 1, 1), (4, 3, 4), (4, 5, 5), (4, 6, 7), (4, 2, 3),
    (3, 4, 0), (4, 0, 3), (4, 1, 2), (4, 3, 5), (4, 4, 5), (4, 5, 6), (4, 6, 8), (4, 2, 4), (4, 0, 4), (4, 1, 3), (3, 5, 0),
    (4, 3, 6), (4, 4, 6), (4, 5, 7), (4, 6, 9), (4, 2, 5), (4, 1, 4), (4, 3, 7), (4, 0, 5), (4, 4, 7), (3, 6, 0), (4, 5, 8),
    (4, 2, 6), (4, 1, 5), (3, 7, 0), (4, 3, 8), (4, 0, 6), (4, 6, 10), (5, 6, 0), (4, 4, 8), (4, 5, 9), (4, 2, 7),
    (4, 1, 6), (4, 3, 9), (4, 0, 7), (4, 4, 9), (5, 4, 0), (4, 2, 8), (4, 1, 7), (4, 5, 10), (5, 5, 0), (4, 0, 8),
    (4, 2, 9), (4, 3, 10), (4, 1, 8), (5, 3, 0), (4, 0, 9), (5, 0, 0), (4, 1, 9), (4, 2, 10), (5, 2, 0), (4, 1, 10),
    (5, 1, 0),
)


def kernel(dims, a_hbm, g_hbm, bi_hbm, bo_hbm, out, a_full, bi, part, sbuf, rbuf, ysend, yrecv, tot, zsend, ytot, rin, g_full, bo,
           pout, sib, ro, oy, rout, rout_t, a_ss, a_rs, gy_s, g_ss, g_rs, rs_ss, rs_rs, y_ss, y_rs, ag_ss, ag_rs, fy_ss, fy_rs,
           ob_s, oy_s, oq_ss, oq_rs, ot_ss, ot_rs, of_ss, of_rs, lsem, out_sem, outv):
    tg, nb = dims
    tk = tg // NG
    ni = nb * NG
    f, e = lax.axis_index("feat"), lax.axis_index("ex")
    z, yh = f // 2, f % 2
    ci, c = e // 2, e % 2
    yl, x = ci // NX, ci % NX
    yo, xm, xp, x2 = 1 - yl, (x + NX - 1) % NX, (x + 1) % NX, (x + 2) % NX
    t2 = 2 * tk

    def dev(z_=z, yh_=yh, yl_=yl, x_=x, c_=c):
        return {"feat": z_ * 2 + yh_, "ex": (yl_ * NX + x_) * 2 + c_}

    def send(src, dst, ss, rs, to):
        return pltpu.make_async_remote_copy(
            src_ref=src, dst_ref=dst, send_sem=ss, recv_sem=rs, device_id=to, device_id_type=MESH
        )

    zp, zm = dev(z_=(z + 1) % NZ), dev(z_=(z + NZ - 1) % NZ)
    zdev = (zp, zm)
    sibling, ypair, yhpair = dev(c_=1 - c), dev(yl_=yo), dev(yh_=1 - yh)
    xpd, xmd = dev(x_=xp), dev(x_=xm)

    barrier = pltpu.get_barrier_semaphore()
    others = [zp, zm, sibling, ypair, yhpair, xpd, xmd, dev(x_=x2)]
    for to in others:
        pl.semaphore_signal(barrier, inc=1, device_id=to, device_id_type=MESH)

    def rows(yl_, x_, c_=c, off=0, size=tk):
        return pl.ds(pl.multiple_of(((yl_ * NX + x_) * 2 + c_) * tk + off, tk // 2), size)

    def half(ref, n, way):
        return ref.at[pl.ds(way * (n // 2), n // 2)]

    ld_bi = pltpu.make_async_copy(bi_hbm, bi, lsem.at[0])
    ld_bo = pltpu.make_async_copy(bo_hbm, bo, lsem.at[1])
    ld_g = pltpu.make_async_copy(g_hbm, g_full.at[z, yh], lsem.at[2])
    ld_a = [
        pltpu.make_async_copy(a_hbm.at[pl.ds(h * tk, tk)], a_full.at[h, rows(yl, x)], lsem.at[3 + h]) for h in range(NG)
    ]
    for ld in (*ld_a, ld_g, ld_bo, ld_bi):
        ld.start()
    pl.semaphore_wait(barrier, len(others))

    hk = tk // 2
    a_out = [
        (rows(yl, x), ypair), (rows(yl, x), xpd), (rows(yl, x), xmd),
        (rows(yl, xm, size=hk), xpd), (rows(yl, xp, off=hk, size=hk), xmd),
        (rows(yo, x), xpd), (rows(yo, x), xmd), (rows(yl, x2), ypair),
    ]
    a_in = [rows(yo, x), rows(yl, xm), rows(yl, xp), rows(yl, x2, size=hk), rows(yl, x2, off=hk, size=hk),
            rows(yo, xm), rows(yo, xp), rows(yo, x2)]
    for s in [(yl, x), (yl, xm), (yl, xp), (yo, x), (yo, xm), (yo, xp), (yl, x2), (yo, x2)]:
        a_out.append((rows(*s), sibling))
        a_in.append(rows(*s, c_=1 - c))

    def a_msg(h, i):
        r, to = a_out[i]
        src = a_hbm.at[pl.ds(h * tk, tk)] if i in (0, 1, 2, 8) else a_full.at[h, r]
        return send(src, a_full.at[h, r], a_ss.at[h, i], a_rs.at[h, i], to)

    def a_wait(h, i, *then):
        r = a_full.at[h, a_in[i]]
        send(r, r, a_ss.at[h, i], a_rs.at[h, i], a_out[i][1]).wait_recv()
        for k in then:
            a_msg(h, k).start()

    def a_first(h):
        for i in (1, 2, 0, 8):
            a_msg(h, i).start()

    def a_done(h):
        ld_a[h].wait()
        for i in range(8, 16):
            a_wait(h, i)

    def ag_region(view, n, s, way, incoming):
        o = (z + NZ - s + (0 if incoming else 1)) if way == 0 else (z + s - (0 if incoming else 1))
        r = view(o % NZ)
        return half(r, n, way) if s == 4 else r

    def ag_copy(view, n, s, way, ss, rs, incoming=False):
        r = ag_region(view, n, s, way, incoming)
        return send(r, r, ss.at[way, s - 1], rs.at[way, s - 1], zdev[way])

    def ag_wait(view, n, s, way, ss, rs):
        ag_copy(view, n, s, way, ss, rs, True).wait_recv()

    def g_args(k):
        j = yh if k == 0 else 1 - yh
        return (lambda o: g_full.at[o, j]), tg, g_ss.at[k], g_rs.at[k]

    def g_copy(k, s, way):
        view, n, ss, rs = g_args(k)
        if k == 0 and s == 1:
            return send(g_hbm, view(z), ss.at[way, 0], rs.at[way, 0], zdev[way])
        return ag_copy(view, n, s, way, ss, rs)

    def g_step(k, s):
        view, n, ss, rs = g_args(k)
        for way in (0, 1):
            if s > 1:
                ag_wait(view, n, s - 1, way, ss, rs)
            if s <= 4:
                g_copy(k, s, way).start()

    gy = send(g_hbm, g_full.at[z, yh], gy_s.at[0], gy_s.at[1], yhpair)

    def is_y(i):
        return functools.reduce(jnp.logical_or, [i == k for k in Y_ITEMS])

    def zsize(kind):
        return t2 if kind == 0 else tk

    def mine(kind, i, o):
        if kind == 0:
            return part[i, o % NZ]
        own = part[i, o % NZ, pl.ds(pl.multiple_of(yh * tk, tk), tk), :]
        return own + yrecv[i, o % NZ].astype(F32)

    def rs_copy(kind, i, s, way):
        n = zsize(kind)
        r = pl.ds(0, n // 2 if s == 1 else n)
        return send(
            sbuf.at[i, way, s - 1, r], rbuf.at[i, way, s - 1, r], rs_ss.at[i, way, s - 1], rs_rs.at[i, way, s - 1], zdev[way]
        )

    def rs_first(kind, i):
        n = zsize(kind)
        whole = mine(kind, i, z + 4)
        for way in (0, 1):
            sbuf[i, way, 0, pl.ds(0, n // 2), :] = whole[way * (n // 2) : (way + 1) * (n // 2)].astype(BF16)
            rs_copy(kind, i, 1, way).start()

    def rs_next(kind, i, s):
        n = zsize(kind)
        m = n // 2
        for way in (0, 1):
            rs_copy(kind, i, s - 1, way).wait_recv()
            own = mine(kind, i, z + NZ - (5 - s) if way else z + (5 - s))
            if s == 2:
                got = rbuf[i, way, 0, pl.ds(0, m), :].astype(F32)
                sbuf[i, way, 1, pl.ds(way * m, m), :] = (own[way * m : (way + 1) * m] + got).astype(BF16)
                sbuf[i, way, 1, pl.ds((1 - way) * m, m), :] = own[(1 - way) * m : (2 - way) * m].astype(BF16)
            else:
                got = rbuf[i, way, s - 2, pl.ds(0, n), :].astype(F32)
                sbuf[i, way, s - 1, pl.ds(0, n), :] = (own + got).astype(BF16)
            rs_copy(kind, i, s, way).start()

    def rs_last(kind, i):
        n = zsize(kind)
        for way in (0, 1):
            rs_copy(kind, i, 4, way).wait_recv()
        got = [rbuf[i, way, 3, pl.ds(0, n), :].astype(F32) for way in (0, 1)]
        return mine(kind, i, z) + got[0] + got[1]

    def view(kind, i):
        if kind == 0:
            return lambda o: rin.at[i, o]
        return lambda o: rin.at[i, o, pl.ds(pl.multiple_of(yh * tk, tk), tk)]

    def ag_step(kind, i, s):
        n = zsize(kind)
        for way in (0, 1):
            if s > 1:
                ag_wait(view(kind, i), n, s - 1, way, ag_ss.at[i], ag_rs.at[i])
            if s <= 4:
                ag_copy(view(kind, i), n, s, way, ag_ss.at[i], ag_rs.at[i]).start()
            if kind == 1 and s > 1:
                fy_copy(i, s - 1, way).start()
        if kind == 1 and s == 1:
            fy_copy(i, 0, 0).start()

    def y_copy(i):
        return send(zsend.at[i], ytot.at[i], y_ss.at[i], y_rs.at[i], yhpair)

    def z_last(i):
        total = rs_last(0, i)
        tot[i] = total
        zsend[i] = total.astype(BF16)
        y_copy(i).start()

    def z_sum(i):
        y_copy(i).wait_recv()
        rin[i, z] = (tot[i] + ytot[i].astype(F32)).astype(BF16)
        ag_step(0, i, 1)

    def yp_copy(i):
        return send(ysend.at[i], yrecv.at[i], y_ss.at[i], y_rs.at[i], yhpair)

    def y_start(i):
        other = pl.ds(pl.multiple_of((1 - yh) * tk, tk), tk)
        for o in range(NZ):
            ysend[i, o] = part[i, o, other, :].astype(BF16)
        yp_copy(i).start()

    def y_sum(i):
        yp_copy(i).wait_recv()
        rs_first(1, i)

    def y_last(i):
        rin[i, z, pl.ds(pl.multiple_of(yh * tk, tk), tk), :] = rs_last(1, i).astype(BF16)
        ag_step(1, i, 1)

    def fy_region(i, s, way, j):
        r = rin.at[i, ((z + s) if way else (z + NZ - s)) % NZ, pl.ds(pl.multiple_of(j * tk, tk), tk)]
        return half(r, tk, way) if s == 4 else r

    def fy_copy(i, s, way, incoming=False):
        r = fy_region(i, s, way, 1 - yh if incoming else yh)
        return send(r, r, fy_ss.at[i, s, way], fy_rs.at[i, s, way], yhpair)

    fy_all = [(0, 0)] + [(s, way) for s in range(1, 5) for way in (0, 1)]

    def y_done(i):
        for s, way in fy_all:
            fy_copy(i, s, way, True).wait_recv()

    def out_copy(b):
        return pltpu.make_async_copy(outv.at[b], out.at[b], out_sem.at[b])

    def correction(b):
        total = None
        spans = 2 * SEQ_LEN // (tg * 2)
        for n in range(rout_t.shape[1] // SEQ_LEN):
            parts = [
                rin[h * nb + b, n * (spans // 2) + k] for h in range(NG) for k in range(spans // 2)
            ]
            per_seq = jnp.dot(
                rout_t[:, n * SEQ_LEN : (n + 1) * SEQ_LEN],
                jnp.concatenate(parts, axis=0),
                preferred_element_type=F32,
            )
            total = per_seq * per_seq if total is None else total + per_seq * per_seq
        outv[b] = total / F32(SEQ_LEN * (rout_t.shape[1] // SEQ_LEN))
        out_copy(b).start()

    ob = send(pout.at[1 - c], sib, ob_s.at[0], ob_s.at[1], sibling)

    def out_partial():
        g_step(0, 5)
        g_step(1, 5)
        ld_g.wait()
        ld_bo.wait()
        for m in range(NZ // 2):
            grads = g_full[2 * m : 2 * m + 2].reshape(4 * tg, g_full.shape[3])
            val = jnp.dot(grads, bo[...], preferred_element_type=F32)
            for k in range(4):
                at = 2 * m + k // 2
                pout[k % 2, at // NX, at % NX] = val[k * tg : (k + 1) * tg]
        ob.start()

    def xplace(d):
        return (x + NX + d) % NX

    def oq_copy(d):
        return send(pout.at[c, :, xplace(d)], ro.at[x], oq_ss.at[d], oq_rs.at[d], dev(x_=xplace(d)))

    def out_pair():
        ob.wait_recv()
        for row in (0, 1):
            for k in range(NX):
                pout[c, row, k] = pout[c, row, k] + sib[row, k]
        for d in range(1, NX):
            oq_copy(d).start()

    def oy_copy():
        return send(pout.at[c, yo, x], oy, oy_s.at[0], oy_s.at[1], ypair)

    def out_row():
        for d in range(1, NX):
            r = ro.at[xplace(-d)]
            send(r, r, oq_ss.at[d], oq_rs.at[d], xpd).wait_recv()
        for row in (0, 1):
            total = pout[c, row, x]
            for d in range(1, NX):
                total = total + ro[xplace(-d), row]
            pout[c, row, x] = total
        oy_copy().start()

    def piece(r, d, c_=c):
        row = yo if r else yl
        return rout.at[pl.ds(pl.multiple_of(((row * NX + xplace(-d)) * 2 + c_) * tg, tg), tg)]

    def ot_copy(r, d):
        src = piece(r, 0)
        return send(src, src, ot_ss.at[r, d], ot_rs.at[r, d], dev(x_=xplace(d)) if d else ypair)

    def ot_wait(r, d):
        dst = piece(r, d) if d else piece(1, 0)
        send(dst, dst, ot_ss.at[r, d], ot_rs.at[r, d], xpd).wait_recv()

    def of_copy(r, d, c_=c):
        src = piece(r, d, c_)
        return send(src, src, of_ss.at[r, d], of_rs.at[r, d], sibling)

    def out_sum():
        oy_copy().wait_recv()
        rout[pl.ds(pl.multiple_of(e * tg, tg), tg), :] = (pout[c, yl, x] + oy[...]).astype(BF16)
        for d in range(NX):
            ot_copy(0, d).start()
        of_copy(0, 0).start()

    def out_forward():
        ot_wait(0, 0)
        of_copy(1, 0).start()
        for d in range(1, NX):
            ot_copy(1, d).start()
        for d in range(1, NX):
            ot_wait(0, d)
            of_copy(0, d).start()

    def out_forward2():
        for d in range(1, NX):
            ot_wait(1, d)
            of_copy(1, d).start()

    def out_done():
        for r in (0, 1):
            for d in range(NX):
                of_copy(r, d, 1 - c).wait_recv()
        for n in range(rout.shape[0] // SEQ_LEN):
            seq = rout[n * SEQ_LEN : (n + 1) * SEQ_LEN, :]
            parts = [
                seq[k * tg + h * tk : k * tg + (h + 1) * tk] for h in range(NG) for k in range(SEQ_LEN // tg)
            ]
            rout_t[:, n * SEQ_LEN : (n + 1) * SEQ_LEN] = jnp.concatenate(parts, axis=0).T

    def product(i):
        b = i % nb
        if (4, i, 0) == first_item:
            ld_bi.wait()
        val = jnp.dot(a_full[i // nb], bi[:, b * BC : (b + 1) * BC], preferred_element_type=F32)
        part[i] = val.reshape(NZ, t2, BC)

    def activations(h, k):
        if k == -1:
            a_first(h)
        elif k == 4:
            a_wait(h, 3)
            a_wait(h, 4, 7, 14)
        elif k == 8:
            a_done(h)
        else:
            a_wait(h, k, *{1: (3, 9), 2: (4, 10), 0: (5, 6, 11), 5: (12,), 6: (13,), 7: (15,)}[k])

    def gradients(k, s):
        if (k, s) == (1, 1):
            r = g_full.at[z, 1 - yh]
            send(r, r, gy_s.at[0], gy_s.at[1], yhpair).wait_recv()
        g_step(k, s)

    def stage(i, k):
        if i in Y_ITEMS:
            if k == 0:
                product(i)
                y_start(i)
            elif k == 1:
                y_sum(i)
            elif k < 5:
                rs_next(1, i, k)
            elif k == 5:
                y_last(i)
            elif k < 10:
                ag_step(1, i, k - 4)
            else:
                y_done(i)
        elif k == 0:
            product(i)
            rs_first(0, i)
        elif k < 4:
            rs_next(0, i, k + 1)
        elif k == 4:
            z_last(i)
        elif k == 5:
            z_sum(i)
        else:
            ag_step(0, i, k - 4)

    out_phases = (out_partial, out_pair, out_row, out_sum, out_forward, out_forward2, out_done)
    first_item = next(op for op in ORDER if op[0] == 4)
    for op, p, q in ORDER:
        if op == 0:
            activations(p, q)
        elif op == 1:
            gy.start()
        elif op == 2:
            gradients(p, q)
        elif op == 3:
            out_phases[p - 1]()
        elif op == 4:
            stage(p, q)
        else:
            correction(p)

    gy.wait_send()
    ob.wait_send()
    for h in range(NG):
        for i in range(16):
            a_msg(h, i).wait_send()
    for k in (0, 1):
        for s in range(1, 5):
            for way in (0, 1):
                g_copy(k, s, way).wait_send()
    oy_copy().wait_send()
    for d in range(NX):
        for r in (0, 1):
            of_copy(r, d).wait_send()
            if d or r == 0:
                ot_copy(r, d).wait_send()
        if d:
            oq_copy(d).wait_send()

    def drain(i, carry):
        for kind in (0, 1):

            @pl.when(is_y(i) == (kind == 1))
            def _():
                for s in range(1, 5):
                    for way in (0, 1):
                        rs_copy(kind, i, s, way).wait_send()
                        ag_copy(view(kind, i), zsize(kind), s, way, ag_ss.at[i], ag_rs.at[i]).wait_send()
                if kind == 0:
                    y_copy(i).wait_send()
                else:
                    yp_copy(i).wait_send()
                    for s, way in fy_all:
                        fy_copy(i, s, way).wait_send()

        return carry

    lax.fori_loop(0, ni, drain, 0)
    for b in range(nb):
        out_copy(b).wait()


def store(blocks, out, held, in_sem, out_sem):
    nb = blocks.shape[0]
    into = [pltpu.make_async_copy(blocks.at[b], held.at[b], in_sem.at[b]) for b in range(nb)]
    back = [pltpu.make_async_copy(held.at[b], out.at[:, pl.ds(b * BC, BC)], out_sem.at[b]) for b in range(nb)]
    for copy in into:
        copy.start()
    for b in range(nb):
        into[b].wait()
        back[b].start()
    for copy in back:
        copy.wait()


def per_device(activations, out_grads, basis_in, basis_out):
    tg, kin = activations.shape
    kout, nout = basis_out.shape
    nin = basis_in.shape[1]
    nb, tokens = nin // BC, tg * 16
    tk, ni = tg // NG, nb * NG
    dma, vmem = pltpu.SemaphoreType.DMA, pltpu.VMEM
    corrected = pl.pallas_call(
        functools.partial(kernel, (tg, nb)),
        out_shape=jax.ShapeDtypeStruct((nb, nout, BC), F32),
        in_specs=[pl.BlockSpec(memory_space=pl.ANY)] * 4,
        out_specs=pl.BlockSpec(memory_space=pltpu.HBM),
        scratch_shapes=[
            vmem((NG, tokens // NG, kin), BF16),
            vmem((kin, nin), BF16),
            vmem((ni, NZ, 2 * tk, BC), F32),
            vmem((ni, 2, 4, 2 * tk, BC), BF16),
            vmem((ni, 2, 4, 2 * tk, BC), BF16),
            vmem((ni, NZ, tk, BC), BF16),
            vmem((ni, NZ, tk, BC), BF16),
            vmem((ni, 2 * tk, BC), F32),
            vmem((ni, 2 * tk, BC), BF16),
            vmem((ni, 2 * tk, BC), BF16),
            vmem((ni, NZ, 2 * tk, BC), BF16),
            vmem((NZ, 2, tg, kout), BF16),
            vmem((kout, nout), BF16),
            vmem((2, 2, NX, tg, nout), F32),
            vmem((2, NX, tg, nout), F32),
            vmem((NX, 2, tg, nout), F32),
            vmem((tg, nout), F32),
            vmem((tokens, nout), BF16),
            vmem((nout, tokens), BF16),
            dma((NG, 16)), dma((NG, 16)), dma((2,)), dma((2, 2, 4)), dma((2, 2, 4)),
            dma((ni, 2, 4)), dma((ni, 2, 4)), dma((ni,)), dma((ni,)), dma((ni, 2, 4)), dma((ni, 2, 4)),
            dma((ni, 5, 2)), dma((ni, 5, 2)),
            dma((2,)), dma((2,)), dma((NX,)), dma((NX,)), dma((2, NX)), dma((2, NX)), dma((2, NX)), dma((2, NX)), dma((3 + NG,)), dma((nb,)),
            vmem((nb, nout, BC), F32),
        ],
        compiler_params=pltpu.CompilerParams(
            collective_id=0, has_side_effects=True, vmem_limit_bytes=58 * 1024 * 1024
        ),
    )(activations, out_grads, basis_in, basis_out)
    return pl.pallas_call(
        store,
        out_shape=jax.ShapeDtypeStruct((nout, nin), F32),
        in_specs=[pl.BlockSpec(memory_space=pltpu.HBM)],
        out_specs=pl.BlockSpec(memory_space=pltpu.HBM),
        scratch_shapes=[vmem((nb, nout, BC), F32), dma((nb,)), dma((nb,))],
    )(corrected)


def solution(mesh):
    return jax.shard_map(
        per_device,
        mesh=mesh,
        in_specs=(P("ex", "feat"), P("feat", "ex"), P("feat", "ex"), P("ex", "feat")),
        out_specs=P("feat", "ex"),
        check_vma=False,
    )
```

```python
import functools

import jax
import jax.numpy as jnp
from jax import lax
from jax.experimental import pallas as pl
from jax.experimental.pallas import tpu as pltpu
from jax.sharding import PartitionSpec as P

SEQ_LEN = 256
BC = 256
NG = 1
MESH = pl.DeviceIdType.MESH
F32, BF16 = jnp.float32, jnp.bfloat16
NZ, NX = 8, 4
Y_ITEMS = (1, 2, 4, 5, 6)
ORDER = (
    (0, 0, -1), (1, 0, 0), (2, 0, 1), (2, 0, 2), (0, 0, 1), (0, 0, 2), (0, 0, 0), (2, 0, 3), (2, 1, 1), (2, 0, 4),
    (0, 0, 4), (2, 1, 2), (2, 1, 3), (0, 0, 5), (0, 0, 6), (0, 0, 7), (2, 1, 4), (0, 0, 8), (4, 6, 0), (4, 5, 0), (3, 1, 0),
    (4, 4, 0), (4, 6, 1), (3, 2, 0), (4, 3, 0), (4, 6, 2), (4, 5, 1), (4, 2, 0), (4, 5, 2), (4, 3, 1), (4, 6, 3), (4, 1, 0),
    (4, 3, 2), (4, 4, 1), (4, 6, 4), (4, 5, 3), (4, 0, 0), (4, 4, 2), (4, 6, 5), (3, 3, 0), (4, 2, 1), (4, 5, 4), (4, 0, 1),
    (4, 6, 6), (4, 4, 3), (4, 2, 2), (4, 1, 1), (4, 5, 5), (4, 3, 3), (4, 0, 2), (4, 6, 7), (3, 4, 0), (4, 4, 4), (4, 1, 2),
    (4, 2, 3), (4, 5, 6), (4, 3, 4), (4, 0, 3), (4, 6, 8), (4, 4, 5), (3, 5, 0), (4, 1, 3), (4, 2, 4), (4, 3, 5), (4, 5, 7),
    (4, 0, 4), (4, 6, 9), (4, 4, 6), (4, 1, 4), (4, 2, 5), (3, 6, 0), (4, 3, 6), (4, 5, 8), (4, 4, 7), (4, 0, 5), (3, 7, 0),
    (4, 1, 5), (4, 2, 6), (4, 4, 8), (4, 6, 10), (4, 3, 7), (4, 5, 9), (5, 6, 0), (4, 1, 6), (4, 0, 6), (4, 2, 7),
    (4, 4, 9), (4, 3, 8), (4, 1, 7), (4, 5, 10), (4, 0, 7), (5, 5, 0), (4, 2, 8), (4, 3, 9), (4, 1, 8), (5, 3, 0),
    (4, 0, 8), (4, 4, 10), (4, 2, 9), (4, 1, 9), (5, 4, 0), (4, 0, 9), (5, 0, 0), (4, 2, 10), (5, 2, 0), (4, 1, 10),
    (5, 1, 0),
)


def kernel(dims, a_hbm, g_hbm, bi_hbm, bo_hbm, out, a_full, bi, part, sbuf, rbuf, ysend, yrecv, tot, zsend, ytot, rin, g_full, bo,
           pout, sib, ro, oy, rout, rout_t, a_ss, a_rs, gy_s, g_ss, g_rs, rs_ss, rs_rs, y_ss, y_rs, ag_ss, ag_rs, fy_ss, fy_rs,
           ob_s, oy_s, oq_ss, oq_rs, ot_ss, ot_rs, of_ss, of_rs, lsem, out_sem, outv):
    tg, nb = dims
    tk = tg // NG
    ni = nb * NG
    f, e = lax.axis_index("feat"), lax.axis_index("ex")
    z, yh = f // 2, f % 2
    ci, c = e // 2, e % 2
    yl, x = ci // NX, ci % NX
    yo, xm, xp, x2 = 1 - yl, (x + NX - 1) % NX, (x + 1) % NX, (x + 2) % NX
    t2 = 2 * tk

    def dev(z_=z, yh_=yh, yl_=yl, x_=x, c_=c):
        return {"feat": z_ * 2 + yh_, "ex": (yl_ * NX + x_) * 2 + c_}

    def send(src, dst, ss, rs, to):
        return pltpu.make_async_remote_copy(
            src_ref=src, dst_ref=dst, send_sem=ss, recv_sem=rs, device_id=to, device_id_type=MESH
        )

    zp, zm = dev(z_=(z + 1) % NZ), dev(z_=(z + NZ - 1) % NZ)
    zdev = (zp, zm)
    sibling, ypair, yhpair = dev(c_=1 - c), dev(yl_=yo), dev(yh_=1 - yh)
    xpd, xmd = dev(x_=xp), dev(x_=xm)

    barrier = pltpu.get_barrier_semaphore()
    others = [zp, zm, sibling, ypair, yhpair, xpd, xmd, dev(x_=x2)]
    for to in others:
        pl.semaphore_signal(barrier, inc=1, device_id=to, device_id_type=MESH)

    def rows(yl_, x_, c_=c, off=0, size=tk):
        return pl.ds(pl.multiple_of(((yl_ * NX + x_) * 2 + c_) * tk + off, tk // 2), size)

    def half(ref, n, way):
        return ref.at[pl.ds(way * (n // 2), n // 2)]

    ld_bi = pltpu.make_async_copy(bi_hbm, bi, lsem.at[0])
    ld_bo = pltpu.make_async_copy(bo_hbm, bo, lsem.at[1])
    ld_g = pltpu.make_async_copy(g_hbm, g_full.at[z, yh], lsem.at[2])
    ld_a = [
        pltpu.make_async_copy(a_hbm.at[pl.ds(h * tk, tk)], a_full.at[h, rows(yl, x)], lsem.at[3 + h]) for h in range(NG)
    ]
    for ld in (*ld_a, ld_g, ld_bo, ld_bi):
        ld.start()
    pl.semaphore_wait(barrier, len(others))

    hk = tk // 2
    a_out = [
        (rows(yl, x), ypair), (rows(yl, x), xpd), (rows(yl, x), xmd),
        (rows(yl, xm, size=hk), xpd), (rows(yl, xp, off=hk, size=hk), xmd),
        (rows(yo, x), xpd), (rows(yo, x), xmd), (rows(yl, x2), ypair),
    ]
    a_in = [rows(yo, x), rows(yl, xm), rows(yl, xp), rows(yl, x2, size=hk), rows(yl, x2, off=hk, size=hk),
            rows(yo, xm), rows(yo, xp), rows(yo, x2)]
    for s in [(yl, x), (yl, xm), (yl, xp), (yo, x), (yo, xm), (yo, xp), (yl, x2), (yo, x2)]:
        a_out.append((rows(*s), sibling))
        a_in.append(rows(*s, c_=1 - c))

    def a_msg(h, i):
        r, to = a_out[i]
        src = a_hbm.at[pl.ds(h * tk, tk)] if i in (0, 1, 2, 8) else a_full.at[h, r]
        return send(src, a_full.at[h, r], a_ss.at[h, i], a_rs.at[h, i], to)

    def a_wait(h, i, *then):
        r = a_full.at[h, a_in[i]]
        send(r, r, a_ss.at[h, i], a_rs.at[h, i], a_out[i][1]).wait_recv()
        for k in then:
            a_msg(h, k).start()

    def a_first(h):
        for i in (1, 2, 0, 8):
            a_msg(h, i).start()

    def a_done(h):
        ld_a[h].wait()
        for i in range(8, 16):
            a_wait(h, i)

    def ag_region(view, n, s, way, incoming):
        o = (z + NZ - s + (0 if incoming else 1)) if way == 0 else (z + s - (0 if incoming else 1))
        r = view(o % NZ)
        return half(r, n, way) if s == 4 else r

    def ag_copy(view, n, s, way, ss, rs, incoming=False):
        r = ag_region(view, n, s, way, incoming)
        return send(r, r, ss.at[way, s - 1], rs.at[way, s - 1], zdev[way])

    def ag_wait(view, n, s, way, ss, rs):
        ag_copy(view, n, s, way, ss, rs, True).wait_recv()

    def g_args(k):
        j = yh if k == 0 else 1 - yh
        return (lambda o: g_full.at[o, j]), tg, g_ss.at[k], g_rs.at[k]

    def g_copy(k, s, way):
        view, n, ss, rs = g_args(k)
        if k == 0 and s == 1:
            return send(g_hbm, view(z), ss.at[way, 0], rs.at[way, 0], zdev[way])
        return ag_copy(view, n, s, way, ss, rs)

    def g_step(k, s):
        view, n, ss, rs = g_args(k)
        for way in (0, 1):
            if s > 1:
                ag_wait(view, n, s - 1, way, ss, rs)
            if s <= 4:
                g_copy(k, s, way).start()

    gy = send(g_hbm, g_full.at[z, yh], gy_s.at[0], gy_s.at[1], yhpair)

    def is_y(i):
        return functools.reduce(jnp.logical_or, [i == k for k in Y_ITEMS])

    def zsize(kind):
        return t2 if kind == 0 else tk

    def mine(kind, i, o):
        if kind == 0:
            return part[i, o % NZ]
        own = part[i, o % NZ, pl.ds(pl.multiple_of(yh * tk, tk), tk), :]
        return own + yrecv[i, o % NZ].astype(F32)

    def rs_copy(kind, i, s, way):
        n = zsize(kind)
        r = pl.ds(0, n // 2 if s == 1 else n)
        return send(
            sbuf.at[i, way, s - 1, r], rbuf.at[i, way, s - 1, r], rs_ss.at[i, way, s - 1], rs_rs.at[i, way, s - 1], zdev[way]
        )

    def rs_first(kind, i):
        n = zsize(kind)
        whole = mine(kind, i, z + 4)
        for way in (0, 1):
            sbuf[i, way, 0, pl.ds(0, n // 2), :] = whole[way * (n // 2) : (way + 1) * (n // 2)].astype(BF16)
            rs_copy(kind, i, 1, way).start()

    def rs_next(kind, i, s):
        n = zsize(kind)
        m = n // 2
        for way in (0, 1):
            rs_copy(kind, i, s - 1, way).wait_recv()
            own = mine(kind, i, z + NZ - (5 - s) if way else z + (5 - s))
            if s == 2:
                got = rbuf[i, way, 0, pl.ds(0, m), :].astype(F32)
                sbuf[i, way, 1, pl.ds(way * m, m), :] = (own[way * m : (way + 1) * m] + got).astype(BF16)
                sbuf[i, way, 1, pl.ds((1 - way) * m, m), :] = own[(1 - way) * m : (2 - way) * m].astype(BF16)
            else:
                got = rbuf[i, way, s - 2, pl.ds(0, n), :].astype(F32)
                sbuf[i, way, s - 1, pl.ds(0, n), :] = (own + got).astype(BF16)
            rs_copy(kind, i, s, way).start()

    def rs_last(kind, i):
        n = zsize(kind)
        for way in (0, 1):
            rs_copy(kind, i, 4, way).wait_recv()
        got = [rbuf[i, way, 3, pl.ds(0, n), :].astype(F32) for way in (0, 1)]
        return mine(kind, i, z) + got[0] + got[1]

    def view(kind, i):
        if kind == 0:
            return lambda o: rin.at[i, o]
        return lambda o: rin.at[i, o, pl.ds(pl.multiple_of(yh * tk, tk), tk)]

    def ag_step(kind, i, s):
        n = zsize(kind)
        for way in (0, 1):
            if s > 1:
                ag_wait(view(kind, i), n, s - 1, way, ag_ss.at[i], ag_rs.at[i])
            if s <= 4:
                ag_copy(view(kind, i), n, s, way, ag_ss.at[i], ag_rs.at[i]).start()
            if kind == 1 and s > 1:
                fy_copy(i, s - 1, way).start()
        if kind == 1 and s == 1:
            fy_copy(i, 0, 0).start()

    def y_copy(i):
        return send(zsend.at[i], ytot.at[i], y_ss.at[i], y_rs.at[i], yhpair)

    def z_last(i):
        total = rs_last(0, i)
        tot[i] = total
        zsend[i] = total.astype(BF16)
        y_copy(i).start()

    def z_sum(i):
        y_copy(i).wait_recv()
        rin[i, z] = (tot[i] + ytot[i].astype(F32)).astype(BF16)
        ag_step(0, i, 1)

    def yp_copy(i):
        return send(ysend.at[i], yrecv.at[i], y_ss.at[i], y_rs.at[i], yhpair)

    def y_start(i):
        other = pl.ds(pl.multiple_of((1 - yh) * tk, tk), tk)
        for o in range(NZ):
            ysend[i, o] = part[i, o, other, :].astype(BF16)
        yp_copy(i).start()

    def y_sum(i):
        yp_copy(i).wait_recv()
        rs_first(1, i)

    def y_last(i):
        rin[i, z, pl.ds(pl.multiple_of(yh * tk, tk), tk), :] = rs_last(1, i).astype(BF16)
        ag_step(1, i, 1)

    def fy_region(i, s, way, j):
        r = rin.at[i, ((z + s) if way else (z + NZ - s)) % NZ, pl.ds(pl.multiple_of(j * tk, tk), tk)]
        return half(r, tk, way) if s == 4 else r

    def fy_copy(i, s, way, incoming=False):
        r = fy_region(i, s, way, 1 - yh if incoming else yh)
        return send(r, r, fy_ss.at[i, s, way], fy_rs.at[i, s, way], yhpair)

    fy_all = [(0, 0)] + [(s, way) for s in range(1, 5) for way in (0, 1)]

    def y_done(i):
        for s, way in fy_all:
            fy_copy(i, s, way, True).wait_recv()

    def out_copy(b):
        return pltpu.make_async_copy(outv.at[b], out.at[b], out_sem.at[b])

    def correction(b):
        total = None
        spans = 2 * SEQ_LEN // (tg * 2)
        for n in range(rout_t.shape[1] // SEQ_LEN):
            parts = [
                rin[h * nb + b, n * (spans // 2) + k] for h in range(NG) for k in range(spans // 2)
            ]
            per_seq = jnp.dot(
                rout_t[:, n * SEQ_LEN : (n + 1) * SEQ_LEN],
                jnp.concatenate(parts, axis=0),
                preferred_element_type=F32,
            )
            total = per_seq * per_seq if total is None else total + per_seq * per_seq
        outv[b] = total / F32(SEQ_LEN * (rout_t.shape[1] // SEQ_LEN))
        out_copy(b).start()

    ob = send(pout.at[1 - c], sib, ob_s.at[0], ob_s.at[1], sibling)

    def out_partial():
        g_step(0, 5)
        g_step(1, 5)
        ld_g.wait()
        ld_bo.wait()
        for m in range(NZ // 2):
            grads = g_full[2 * m : 2 * m + 2].reshape(4 * tg, g_full.shape[3])
            val = jnp.dot(grads, bo[...], preferred_element_type=F32)
            for k in range(4):
                at = 2 * m + k // 2
                pout[k % 2, at // NX, at % NX] = val[k * tg : (k + 1) * tg]
        ob.start()

    def xplace(d):
        return (x + NX + d) % NX

    def oq_copy(d):
        return send(pout.at[c, :, xplace(d)], ro.at[x], oq_ss.at[d], oq_rs.at[d], dev(x_=xplace(d)))

    def out_pair():
        ob.wait_recv()
        for row in (0, 1):
            for k in range(NX):
                pout[c, row, k] = pout[c, row, k] + sib[row, k]
        for d in range(1, NX):
            oq_copy(d).start()

    def oy_copy():
        return send(pout.at[c, yo, x], oy, oy_s.at[0], oy_s.at[1], ypair)

    def out_row():
        for d in range(1, NX):
            r = ro.at[xplace(-d)]
            send(r, r, oq_ss.at[d], oq_rs.at[d], xpd).wait_recv()
        for row in (0, 1):
            total = pout[c, row, x]
            for d in range(1, NX):
                total = total + ro[xplace(-d), row]
            pout[c, row, x] = total
        oy_copy().start()

    def piece(r, d, c_=c):
        row = yo if r else yl
        return rout.at[pl.ds(pl.multiple_of(((row * NX + xplace(-d)) * 2 + c_) * tg, tg), tg)]

    def ot_copy(r, d):
        src = piece(r, 0)
        return send(src, src, ot_ss.at[r, d], ot_rs.at[r, d], dev(x_=xplace(d)) if d else ypair)

    def ot_wait(r, d):
        dst = piece(r, d) if d else piece(1, 0)
        send(dst, dst, ot_ss.at[r, d], ot_rs.at[r, d], xpd).wait_recv()

    def of_copy(r, d, c_=c):
        src = piece(r, d, c_)
        return send(src, src, of_ss.at[r, d], of_rs.at[r, d], sibling)

    def out_sum():
        oy_copy().wait_recv()
        rout[pl.ds(pl.multiple_of(e * tg, tg), tg), :] = (pout[c, yl, x] + oy[...]).astype(BF16)
        for d in range(NX):
            ot_copy(0, d).start()
        of_copy(0, 0).start()

    def out_forward():
        ot_wait(0, 0)
        of_copy(1, 0).start()
        for d in range(1, NX):
            ot_copy(1, d).start()
        for d in range(1, NX):
            ot_wait(0, d)
            of_copy(0, d).start()

    def out_forward2():
        for d in range(1, NX):
            ot_wait(1, d)
            of_copy(1, d).start()

    def out_done():
        for r in (0, 1):
            for d in range(NX):
                of_copy(r, d, 1 - c).wait_recv()
        for n in range(rout.shape[0] // SEQ_LEN):
            seq = rout[n * SEQ_LEN : (n + 1) * SEQ_LEN, :]
            parts = [
                seq[k * tg + h * tk : k * tg + (h + 1) * tk] for h in range(NG) for k in range(SEQ_LEN // tg)
            ]
            rout_t[:, n * SEQ_LEN : (n + 1) * SEQ_LEN] = jnp.concatenate(parts, axis=0).T

    def product(i):
        b = i % nb
        if (4, i, 0) == first_item:
            ld_bi.wait()
        val = jnp.dot(a_full[i // nb], bi[:, b * BC : (b + 1) * BC], preferred_element_type=F32)
        part[i] = val.reshape(NZ, t2, BC)

    def activations(h, k):
        if k == -1:
            a_first(h)
        elif k == 4:
            a_wait(h, 3)
            a_wait(h, 4, 7, 14)
        elif k == 8:
            a_done(h)
        else:
            a_wait(h, k, *{1: (3, 9), 2: (4, 10), 0: (5, 6, 11), 5: (12,), 6: (13,), 7: (15,)}[k])

    def gradients(k, s):
        if (k, s) == (1, 1):
            r = g_full.at[z, 1 - yh]
            send(r, r, gy_s.at[0], gy_s.at[1], yhpair).wait_recv()
        g_step(k, s)

    def stage(i, k):
        if i in Y_ITEMS:
            if k == 0:
                product(i)
                y_start(i)
            elif k == 1:
                y_sum(i)
            elif k < 5:
                rs_next(1, i, k)
            elif k == 5:
                y_last(i)
            elif k < 10:
                ag_step(1, i, k - 4)
            else:
                y_done(i)
        elif k == 0:
            product(i)
            rs_first(0, i)
        elif k < 4:
            rs_next(0, i, k + 1)
        elif k == 4:
            z_last(i)
        elif k == 5:
            z_sum(i)
        else:
            ag_step(0, i, k - 4)

    out_phases = (out_partial, out_pair, out_row, out_sum, out_forward, out_forward2, out_done)
    first_item = next(op for op in ORDER if op[0] == 4)
    for op, p, q in ORDER:
        if op == 0:
            activations(p, q)
        elif op == 1:
            gy.start()
        elif op == 2:
            gradients(p, q)
        elif op == 3:
            out_phases[p - 1]()
        elif op == 4:
            stage(p, q)
        else:
            correction(p)

    gy.wait_send()
    ob.wait_send()
    for h in range(NG):
        for i in range(16):
            a_msg(h, i).wait_send()
    for k in (0, 1):
        for s in range(1, 5):
            for way in (0, 1):
                g_copy(k, s, way).wait_send()
    oy_copy().wait_send()
    for d in range(NX):
        for r in (0, 1):
            of_copy(r, d).wait_send()
            if d or r == 0:
                ot_copy(r, d).wait_send()
        if d:
            oq_copy(d).wait_send()

    def drain(i, carry):
        for kind in (0, 1):

            @pl.when(is_y(i) == (kind == 1))
            def _():
                for s in range(1, 5):
                    for way in (0, 1):
                        rs_copy(kind, i, s, way).wait_send()
                        ag_copy(view(kind, i), zsize(kind), s, way, ag_ss.at[i], ag_rs.at[i]).wait_send()
                if kind == 0:
                    y_copy(i).wait_send()
                else:
                    yp_copy(i).wait_send()
                    for s, way in fy_all:
                        fy_copy(i, s, way).wait_send()

        return carry

    lax.fori_loop(0, ni, drain, 0)
    for b in range(nb):
        out_copy(b).wait()


def store(blocks, out, held, in_sem, out_sem):
    nb = blocks.shape[0]
    into = [pltpu.make_async_copy(blocks.at[b], held.at[b], in_sem.at[b]) for b in range(nb)]
    back = [pltpu.make_async_copy(held.at[b], out.at[:, pl.ds(b * BC, BC)], out_sem.at[b]) for b in range(nb)]
    for copy in into:
        copy.start()
    for b in range(nb):
        into[b].wait()
        back[b].start()
    for copy in back:
        copy.wait()


def per_device(activations, out_grads, basis_in, basis_out):
    tg, kin = activations.shape
    kout, nout = basis_out.shape
    nin = basis_in.shape[1]
    nb, tokens = nin // BC, tg * 16
    tk, ni = tg // NG, nb * NG
    dma, vmem = pltpu.SemaphoreType.DMA, pltpu.VMEM
    corrected = pl.pallas_call(
        functools.partial(kernel, (tg, nb)),
        out_shape=jax.ShapeDtypeStruct((nb, nout, BC), F32),
        in_specs=[pl.BlockSpec(memory_space=pl.ANY)] * 4,
        out_specs=pl.BlockSpec(memory_space=pltpu.HBM),
        scratch_shapes=[
            vmem((NG, tokens // NG, kin), BF16),
            vmem((kin, nin), BF16),
            vmem((ni, NZ, 2 * tk, BC), F32),
            vmem((ni, 2, 4, 2 * tk, BC), BF16),
            vmem((ni, 2, 4, 2 * tk, BC), BF16),
            vmem((ni, NZ, tk, BC), BF16),
            vmem((ni, NZ, tk, BC), BF16),
            vmem((ni, 2 * tk, BC), F32),
            vmem((ni, 2 * tk, BC), BF16),
            vmem((ni, 2 * tk, BC), BF16),
            vmem((ni, NZ, 2 * tk, BC), BF16),
            vmem((NZ, 2, tg, kout), BF16),
            vmem((kout, nout), BF16),
            vmem((2, 2, NX, tg, nout), F32),
            vmem((2, NX, tg, nout), F32),
            vmem((NX, 2, tg, nout), F32),
            vmem((tg, nout), F32),
            vmem((tokens, nout), BF16),
            vmem((nout, tokens), BF16),
            dma((NG, 16)), dma((NG, 16)), dma((2,)), dma((2, 2, 4)), dma((2, 2, 4)),
            dma((ni, 2, 4)), dma((ni, 2, 4)), dma((ni,)), dma((ni,)), dma((ni, 2, 4)), dma((ni, 2, 4)),
            dma((ni, 5, 2)), dma((ni, 5, 2)),
            dma((2,)), dma((2,)), dma((NX,)), dma((NX,)), dma((2, NX)), dma((2, NX)), dma((2, NX)), dma((2, NX)), dma((3 + NG,)), dma((nb,)),
            vmem((nb, nout, BC), F32),
        ],
        compiler_params=pltpu.CompilerParams(
            collective_id=0, has_side_effects=True, vmem_limit_bytes=58 * 1024 * 1024
        ),
    )(activations, out_grads, basis_in, basis_out)
    return pl.pallas_call(
        store,
        out_shape=jax.ShapeDtypeStruct((nout, nin), F32),
        in_specs=[pl.BlockSpec(memory_space=pltpu.HBM)],
        out_specs=pl.BlockSpec(memory_space=pltpu.HBM),
        scratch_shapes=[vmem((nb, nout, BC), F32), dma((nb,)), dma((nb,))],
    )(corrected)


def solution(mesh):
    return jax.shard_map(
        per_device,
        mesh=mesh,
        in_specs=(P("ex", "feat"), P("feat", "ex"), P("feat", "ex"), P("ex", "feat")),
        out_specs=P("feat", "ex"),
        check_vma=False,
    )
```
